256 devices in a mesh: date: 16 (over z, core), path: 16 (over x, y).
Axes of the slice: x: 4, y: 4, z: 8, core: 2. Of those that a mesh axis runs over, the one named last changes fastest.
Arguments:
- features: bfloat16 [32, 2048, 2048], P('date', 'path'), may hold values from -6 to 6
- payoff: float32 [32, 2048, 256], P('date', 'path'), may hold values from -8 to 64
- coefficients: bfloat16 [2048, 256], replicated, may hold values from -0.02734375 to 0.02734375
- exercise: int32 [32, 256], P('date'), may hold values from 0 to 1, as said below
Outputs:
- gradient: float32 [2048, 256], P(('date', 'path'))
- bound: float32 [256], replicated
- spread: float32 [256], replicated
The draws below stay inside these ranges and needn't reach their ends.
Inputs may be any that keep to these rules, and one draw needn't show every extreme that they name: `exercise`: every contract may be exercised at the first and at the last date.
All inputs are finite; a program needn't handle non-finite values.
Results may differ from the reference program's by a relative error of at most 0.0017.
Values sent between devices are 32-bit elements; how exact they have to be, the bound alone decides.
A program may use at most 64 MiB of HBM per device.

```python
import jax
import jax.numpy as jnp

K = 2048
C = 256
DATES = 32
PATHS = 2048


def draw_payoff(key, part):
    first = jax.random.fold_in(key, 0)
    return jax.random.normal(first, (DATES, PATHS, C), jnp.float32)


def draw_exercise(key, part):
    levels = jax.random.randint(jax.random.fold_in(key, 7), (DATES, C), 0, 4)
    dates = jnp.arange(DATES)[:, None]
    edges = (dates == 0) | (dates == DATES - 1)
    return jnp.where(edges | (levels > 0), 1, 0).astype(jnp.int32)


def spiked(drawn, key, source, target, blocks, factor):
    def block_of(axis_at):
        return (jnp.arange(drawn.shape[axis_at]) // (drawn.shape[axis_at] // blocks)).reshape((-1,) + (1,) * (drawn.ndim - 1 - axis_at))

    first = jax.random.permutation(key, blocks)[block_of(target)]
    second = (block_of(target) + blocks // 2) % blocks
    return jnp.where((block_of(source) == first) | (block_of(source) == second), factor * drawn, drawn)


def block_levels(own_key, shape, pieces, low, high):
    def one(position, blocks):
        steps = jax.random.uniform(jax.random.fold_in(jax.random.fold_in(own_key, 6), position), (blocks,), jnp.float32, low / len(pieces), high / len(pieces))
        return jnp.repeat(jnp.exp(steps), shape[position] // blocks).reshape((-1,) + (1,) * (len(shape) - position - 1))

    level = one(*pieces[0])
    for cut in pieces[1:]:
        level = level * one(*cut)
    return level


def centred(rng, shape, scale, most, cuts=(), kind=jnp.bfloat16):
    loudness = block_levels(rng, shape, cuts, -0.22, 0.18) if cuts else 1.0
    result = jax.random.normal(rng, shape, jnp.float32) * scale * loudness
    return jnp.minimum(jnp.maximum(result, -most), most).astype(kind)


def bell_draw_with(own_key, extent, deviation, reach, pieces, heavy, dtype=jnp.bfloat16):
    entries = deviation * jax.random.normal(own_key, extent, jnp.float32)
    if pieces:
        entries = entries * block_levels(own_key, extent, pieces, -0.22, 0.18)
    return jnp.clip(spiked(entries, jax.random.fold_in(own_key, 3), *heavy), -reach, reach).astype(dtype)


def setup_inputs(seed: int = 0) -> dict:
    seeds = jax.random.split(jax.random.key(seed), 5)
    features = bell_draw_with(seeds[0], (DATES, PATHS, K), 1.0, 6.0, ((0, 16), (1, 16)), (1, 2, 16, 2.0))
    payoff = draw_payoff(jax.random.fold_in(seeds[4], 71), 0)
    coefficients = centred(seeds[2], (K, C), (25 * K) ** -0.5, 0.02734375)
    exercise = draw_exercise(jax.random.fold_in(seeds[4], 71), 0)
    return dict(features=features, payoff=payoff, coefficients=coefficients, exercise=exercise)


TEMP = 0.25
NEG = -1e30


def reference(features, payoff, coefficients, exercise):
    flat = features.reshape(-1, K)
    increments = jnp.dot(flat, coefficients, preferred_element_type=jnp.float32).reshape(DATES, PATHS, C)
    martingale = jnp.cumsum(increments, axis=0)
    allowed = exercise[:, None, :] > 0
    score = jnp.where(allowed, (payoff - martingale) / TEMP, NEG)
    peak = jnp.max(score, axis=0)
    shifted = jnp.exp(score - peak[None])
    total = jnp.sum(shifted, axis=0)
    smoothed = TEMP * (peak + jnp.log(total))
    weight = shifted / total[None]
    tail = jnp.flip(jnp.cumsum(jnp.flip(weight, 0), axis=0), 0).astype(jnp.bfloat16)
    gradient = -jnp.dot(flat.T, tail.reshape(-1, C), preferred_element_type=jnp.float32) / PATHS
    bound = jnp.sum(smoothed, axis=0) / PATHS
    spread = jnp.sum(smoothed * smoothed, axis=0) / PATHS - bound * bound
    return gradient, bound, spread
```

```python
import functools

import jax
import jax.numpy as jnp
from jax import lax
from jax.experimental import pallas as pl
from jax.experimental.pallas import tpu as pltpu
from jax.sharding import Mesh
from jax.sharding import PartitionSpec as P

DATE = ("z", "core")
PATH = ("x", "y")
AXES = ("z", "core", "x", "y")
NZ, NC, NX, NY = 8, 2, 4, 4
ND = NZ * NC
TEMP = 0.25
MASKED = -1e30 * TEMP
PATHS = 2048
K = 2048
C = 256
R = 8
F32 = jnp.float32
BF16 = jnp.bfloat16
MESH = pl.DeviceIdType.MESH


def body(
    feat,
    pay,
    coef,
    exer,
    grad,
    bound,
    spread,
    fbuf,
    cbuf,
    pbuf,
    ebuf,
    mpay,
    inc,
    pay_all,
    inc_all,
    tail_all,
    tail_in,
    ft,
    other_part,
    other_got,
    part,
    got1,
    sum1,
    got2,
    sum2,
    got3,
    stat,
    stat_c,
    stat_1,
    stat_2,
    stat_3,
    load_sem,
    pay_s,
    pay_r,
    inc_s,
    inc_r,
    tail_s,
    tail_r,
    half_s,
    half_r,
    one_s,
    one_r,
    two_s,
    two_r,
    three_s,
    three_r,
    stat_s,
    stat_r,
):
    z, core, x, y = (lax.axis_index(a) for a in AXES)
    d = z * NC + core
    other = 1 - core

    loads = [
        pltpu.make_async_copy(pay, pbuf, load_sem.at[0]),
        pltpu.make_async_copy(exer, ebuf, load_sem.at[1]),
        pltpu.make_async_copy(coef, cbuf, load_sem.at[2]),
        pltpu.make_async_copy(feat, fbuf, load_sem.at[3]),
    ]
    for copy in loads:
        copy.start()

    def date_peer(i):
        e = lax.rem(d + i, ND)
        return e, (e // NC, lax.rem(e, NC), x, y)

    a = (1 - core) * x + core * y
    b = (1 - core) * y + core * x

    def first_peer(i):
        e = lax.rem(a + i, NX)
        return e, (z, core, (1 - core) * e + core * x, (1 - core) * y + core * e)

    def second_peer(i):
        e = lax.rem(b + i, NX)
        return e, (z, core, (1 - core) * x + core * e, (1 - core) * e + core * y)

    def third_peer(i):
        e = lax.rem(z + i, NZ)
        return e, (e, core, x, y)

    def x_peer(i):
        e = lax.rem(x + i, NX)
        return e, (z, core, e, y)

    def y_peer(i):
        e = lax.rem(y + i, NY)
        return e, (z, core, x, e)

    barrier = pltpu.get_barrier_semaphore()

    @pl.loop(1, ND)
    def _(i):
        pl.semaphore_signal(barrier, inc=1, device_id=date_peer(i)[1], device_id_type=MESH)

    @pl.loop(1, NX)
    def _(i):
        pl.semaphore_signal(barrier, inc=1, device_id=first_peer(i)[1], device_id_type=MESH)
        pl.semaphore_signal(barrier, inc=1, device_id=second_peer(i)[1], device_id_type=MESH)

    loads[0].wait()
    loads[1].wait()
    for t in range(2):
        mpay[t] = jnp.where(ebuf[t : t + 1] > 0, pbuf[t], MASKED)

    pl.semaphore_wait(barrier, ND - 1 + 2 * (NX - 1))

    def mine(ref, e):
        return ref.at[:, pl.ds(pl.multiple_of(e * R, R), R), :]

    def date_copy(src, dst, ssem, rsem, i):
        e, dev = date_peer(i)
        return pltpu.make_async_remote_copy(
            src(e), dst, ssem.at[i - 1], rsem.at[i - 1], device_id=dev, device_id_type=MESH
        )

    def date_wait(src, dst, ssem, rsem, i):
        dev = date_peer(i)[1]
        return pltpu.make_async_remote_copy(
            src(date_peer(i)[0]), dst(lax.rem(d + ND - i, ND)), ssem.at[i - 1], rsem.at[i - 1], device_id=dev, device_id_type=MESH
        )

    @pl.loop(1, ND)
    def _(i):
        date_copy(lambda e: mine(mpay, e), pay_all.at[d], pay_s, pay_r, i).start()

    loads[2].wait()
    loads[3].wait()
    inc[...] = jnp.dot(fbuf[...].reshape(2 * 128, K), cbuf[...], preferred_element_type=F32).reshape(2, 128, C)

    @pl.loop(1, ND)
    def _(i):
        date_copy(lambda e: mine(inc, e), inc_all.at[d], inc_s, inc_r, i).start()

    here = pl.ds(pl.multiple_of(d * R, R), R)
    pay_all[d] = mpay[:, here, :]
    inc_all[d] = inc[:, here, :]

    for k in range(8):
        strip = fbuf[:, :, k * 256 : (k + 1) * 256].reshape(256, 256)
        ft[k * 256 : (k + 1) * 256, :] = strip.T

    @pl.loop(1, ND)
    def _(i):
        date_wait(lambda e: mine(mpay, e), lambda e: pay_all.at[e], pay_s, pay_r, i).wait_recv()
        date_wait(lambda e: mine(inc, e), lambda e: inc_all.at[e], inc_s, inc_r, i).wait_recv()

    total = jnp.zeros((R, C), F32)
    scores = []
    peak = None
    for t in range(2 * ND):
        total = total + inc_all[t // 2, t % 2]
        score = (pay_all[t // 2, t % 2] - total) / TEMP
        peak = score if peak is None else jnp.maximum(peak, score)
        scores.append(score)
    weights = [jnp.exp(s - peak) for s in scores]
    total = functools.reduce(lambda p, q: p + q, weights)
    scale = 1.0 / total
    run = jnp.zeros((R, C), F32)
    for t in reversed(range(2 * ND)):
        run = run + weights[t] * scale
        tail_all[t // 2, t % 2] = run
    smoothed = TEMP * (peak + jnp.log(total))
    stat[0] = jnp.zeros((R, C), F32)
    stat[0, 0:1] = jnp.sum(smoothed, axis=0, keepdims=True)
    stat[0, 1:2] = jnp.sum(smoothed * smoothed, axis=0, keepdims=True)

    @pl.loop(1, ND)
    def _(i):
        date_copy(lambda e: tail_all.at[e], mine(tail_in, d), tail_s, tail_r, i).start()

    tail_in[:, here, :] = tail_all[d]
    partner = (z, other, x, y)
    pair = pltpu.make_async_remote_copy(
        stat.at[0], stat_c, stat_s.at[0], stat_r.at[0], device_id=partner, device_id_type=MESH
    )
    pair.start()

    @pl.loop(1, ND)
    def _(i):
        date_wait(lambda e: tail_all.at[e], lambda e: mine(tail_in, e), tail_s, tail_r, i).wait_recv()

    tail = tail_in[...].reshape(256, C).astype(BF16)

    def half_copy(k):
        return pltpu.make_async_remote_copy(
            other_part.at[k], other_got.at[k], half_s.at[k], half_r.at[k], device_id=partner, device_id_type=MESH
        )

    def product(k, which, out):
        rows = ft[pl.ds(pl.multiple_of(k * 256 + which * 128, 128), 128), :]
        block = jnp.dot(rows, tail, preferred_element_type=F32)
        for p in range(NX):
            for q in range(NY):
                n = (p * NY + q) * R
                out[k, (1 - which) * p + which * q, (1 - which) * q + which * p] = block[n : n + R]

    @pl.loop(0, NZ)
    def _(k):
        product(k, other, other_part)
        half_copy(k).start()

    @pl.loop(0, NZ)
    def _(k):
        product(k, core, part)

    pair.wait_recv()
    stat[1] = stat[0] + stat_c[...]

    @pl.loop(0, NZ)
    def _(k):
        half_copy(k).wait_recv()
        part[k] = part[k] + other_got[k]

    def one_copy(i):
        e, dev = first_peer(i)
        return pltpu.make_async_remote_copy(
            part.at[:, e], got1.at[i - 1], one_s.at[i - 1], one_r.at[i - 1], device_id=dev, device_id_type=MESH
        )

    def two_copy(i):
        e, dev = second_peer(i)
        return pltpu.make_async_remote_copy(
            sum1.at[:, e], got2.at[i - 1], two_s.at[i - 1], two_r.at[i - 1], device_id=dev, device_id_type=MESH
        )

    def three_copy(i):
        e, dev = third_peer(i)
        return pltpu.make_async_remote_copy(
            sum2.at[e], got3.at[i - 1], three_s.at[i - 1], three_r.at[i - 1], device_id=dev, device_id_type=MESH
        )

    def stat_copy(level, got, peer, slot, base, i):
        return pltpu.make_async_remote_copy(
            stat.at[level], got.at[slot], stat_s.at[base + i], stat_r.at[base + i], device_id=peer(i)[1], device_id_type=MESH
        )

    def stat_x(i, arriving=False):
        return stat_copy(1, stat_1, x_peer, lax.rem(x + NX - i, NX) if arriving else x, 0, i)

    def stat_y(i, arriving=False):
        return stat_copy(2, stat_2, y_peer, lax.rem(y + NY - i, NY) if arriving else y, 3, i)

    def stat_z(i, arriving=False):
        return stat_copy(3, stat_3, third_peer, lax.rem(z + NZ - i, NZ) if arriving else z, 6, i)

    def summed(got, n):
        return functools.reduce(lambda p, q: p + q, [got[i] for i in range(n)])

    @pl.loop(1, NX)
    def _(i):
        one_copy(i).start()
        stat_x(i).start()

    @pl.loop(1, NX)
    def _(i):
        one_copy(i).wait_recv()
        stat_x(i, True).wait_recv()

    sum1[...] = ((part[:, a] + got1[0]) + got1[1]) + got1[2]
    stat_1[x] = stat[1]
    stat[2] = summed(stat_1, NX)

    @pl.loop(1, NX)
    def _(i):
        two_copy(i).start()
        stat_y(i).start()

    @pl.loop(1, NX)
    def _(i):
        two_copy(i).wait_recv()
        stat_y(i, True).wait_recv()

    sum2[...] = ((sum1[:, b] + got2[0]) + got2[1]) + got2[2]
    stat_2[y] = stat[2]
    stat[3] = summed(stat_2, NY)

    @pl.loop(1, NZ)
    def _(i):
        three_copy(i).start()
        stat_z(i).start()

    @pl.loop(1, NZ)
    def _(i):
        three_copy(i).wait_recv()
        stat_z(i, True).wait_recv()

    total = sum2[z]
    for i in range(NZ - 1):
        total = total + got3[i]
    stat_3[z] = stat[3]
    sums = summed(stat_3, NZ)
    grad[...] = total * (-1.0 / PATHS)
    mean = sums[0:1] * (1.0 / PATHS)
    bound[...] = mean
    spread[...] = sums[1:2] * (1.0 / PATHS) - mean * mean

    @pl.loop(1, ND)
    def _(i):
        date_copy(lambda e: mine(mpay, e), pay_all.at[d], pay_s, pay_r, i).wait_send()
        date_copy(lambda e: mine(inc, e), inc_all.at[d], inc_s, inc_r, i).wait_send()
        date_copy(lambda e: tail_all.at[e], mine(tail_in, d), tail_s, tail_r, i).wait_send()

    pair.wait_send()

    @pl.loop(0, NZ)
    def _(k):
        half_copy(k).wait_send()

    @pl.loop(1, NX)
    def _(i):
        one_copy(i).wait_send()
        two_copy(i).wait_send()
        stat_x(i).wait_send()
        stat_y(i).wait_send()

    @pl.loop(1, NZ)
    def _(i):
        three_copy(i).wait_send()
        stat_z(i).wait_send()


def shards(features, payoff, coefficients, exercise):
    dma = pltpu.SemaphoreType.DMA
    vmem = pltpu.VMEM
    grad, bound, spread = pl.pallas_call(
        body,
        name="dual_bound",
        out_shape=(
            jax.ShapeDtypeStruct((R, C), F32),
            jax.ShapeDtypeStruct((1, C), F32),
            jax.ShapeDtypeStruct((1, C), F32),
        ),
        in_specs=[pl.BlockSpec(memory_space=pl.ANY)] * 4,
        out_specs=[pl.BlockSpec(memory_space=pltpu.VMEM)] * 3,
        scratch_shapes=[
            vmem((2, 128, K), BF16),
            vmem((K, C), BF16),
            vmem((2, 128, C), F32),
            vmem((2, C), jnp.int32),
            vmem((2, 128, C), F32),
            vmem((2, 128, C), F32),
            vmem((ND, 2, R, C), F32),
            vmem((ND, 2, R, C), F32),
            vmem((ND, 2, R, C), F32),
            vmem((2, 128, C), F32),
            vmem((K, 256), BF16),
            vmem((NZ, NX, NY, R, C), F32),
            vmem((NZ, NX, NY, R, C), F32),
            vmem((NZ, NX, NY, R, C), F32),
            vmem((NX - 1, NZ, NY, R, C), F32),
            vmem((NZ, NY, R, C), F32),
            vmem((NY - 1, NZ, R, C), F32),
            vmem((NZ, R, C), F32),
            vmem((NZ - 1, R, C), F32),
            vmem((4, R, C), F32),
            vmem((R, C), F32),
            vmem((NX, R, C), F32),
            vmem((NY, R, C), F32),
            vmem((NZ, R, C), F32),
            dma((4,)),
            dma((ND - 1,)),
            dma((ND - 1,)),
            dma((ND - 1,)),
            dma((ND - 1,)),
            dma((ND - 1,)),
            dma((ND - 1,)),
            dma((NZ,)),
            dma((NZ,)),
            dma((NX - 1,)),
            dma((NX - 1,)),
            dma((NY - 1,)),
            dma((NY - 1,)),
            dma((NZ - 1,)),
            dma((NZ - 1,)),
            dma((14,)),
            dma((14,)),
        ],
        compiler_params=pltpu.CompilerParams(
            collective_id=0, has_side_effects=True, vmem_limit_bytes=40 * 1024 * 1024
        ),
    )(features, payoff, coefficients, exercise)
    return grad, bound.reshape(C), spread.reshape(C)


def solution(mesh):
    torus = Mesh(mesh.devices.reshape(NZ, NC, NX, NY), AXES)
    in_specs = (P(DATE, PATH, None), P(DATE, PATH, None), P(), P(DATE, None))
    out_specs = (P(DATE + PATH, None), P(), P())
    return jax.shard_map(
        shards, mesh=torus, in_specs=in_specs, out_specs=out_specs, check_vma=False
    )
```

```python
import functools

import jax
import jax.numpy as jnp
from jax import lax
from jax.experimental import pallas as pl
from jax.experimental.pallas import tpu as pltpu
from jax.sharding import Mesh
from jax.sharding import PartitionSpec as P

DATE = ("z", "core")
PATH = ("x", "y")
AXES = ("z", "core", "x", "y")
NZ, NC, NX, NY = 8, 2, 4, 4
TEMP = 0.25
MASKED = -1e30 * TEMP
PATHS = 2048
K = 2048
C = 256
R = 8
H = 2
W = C // H
F32 = jnp.float32
BF16 = jnp.bfloat16
MESH = pl.DeviceIdType.MESH
ORDER = (2, 1, 3, 0)


def scope(name):
    return jax.named_scope(name)


def body(
    feat,
    pay,
    coef,
    exer,
    grad,
    sums_out,
    fbuf,
    cbuf,
    pbuf,
    ebuf,
    mpay,
    pay_got,
    inc,
    inc_got,
    fx_send,
    fx_got,
    fall,
    ft,
    rel,
    bl,
    bl_all,
    fl,
    fl_in,
    other_part,
    other_got,
    part,
    via_l,
    via_r,
    got_l,
    got_r,
    sum1,
    got2,
    sum2,
    got3,
    stat,
    stat_c,
    stat_1,
    stat_2,
    stat_3,
    load_sem,
    pair_s,
    pair_r,
    bl_s,
    bl_r,
    fl_s,
    fl_r,
    half_s,
    half_r,
    one_s,
    one_r,
    two_s,
    two_r,
    three_s,
    three_r,
    stat_s,
    stat_r,
):
    z, core, x, y = (lax.axis_index(a) for a in AXES)
    other = 1 - core

    loads = [
        pltpu.make_async_copy(coef, cbuf, load_sem.at[0]),
        pltpu.make_async_copy(feat, fbuf, load_sem.at[1]),
        pltpu.make_async_copy(exer, ebuf, load_sem.at[2]),
        pltpu.make_async_copy(pay, pbuf, load_sem.at[3]),
    ]
    for copy in loads:
        copy.start()

    a = (1 - core) * x + core * y
    b = (1 - core) * y + core * x
    a_other = (1 - other) * x + other * y

    def along_a(e):
        return (z, core, (1 - core) * e + core * x, (1 - core) * y + core * e)

    def along_b(e):
        return (z, core, (1 - core) * x + core * e, (1 - core) * e + core * y)

    partner = (z, other, x, y)
    right, left = along_a(lax.rem(a + 1, NX)), along_a(lax.rem(a + NX - 1, NX))

    def b_peer(i):
        e = lax.rem(b + i, NX)
        return e, along_b(e)

    def z_peer(i):
        e = lax.rem(z + i, NZ)
        return e, (e, core, x, y)

    def x_peer(i):
        e = lax.rem(x + i, NX)
        return e, (z, core, e, y)

    def y_peer(i):
        e = lax.rem(y + i, NY)
        return e, (z, core, x, e)

    def remote(src, dst, ssem, rsem, device):
        return pltpu.make_async_remote_copy(src, dst, ssem, rsem, device_id=device, device_id_type=MESH)

    def greet(device):
        pl.semaphore_signal(barrier, inc=1, device_id=device, device_id_type=MESH)

    barrier = pltpu.get_barrier_semaphore()
    with scope("a_signal"):
        greet(partner)

        @pl.loop(1, NZ)
        def _(i):
            greet(z_peer(i)[1])

        @pl.loop(1, NX)
        def _(i):
            greet(x_peer(i)[1])
            greet(y_peer(i)[1])

    with scope("b_mm1"):
        loads[0].wait()
        loads[1].wait()
        flat = fbuf[...].reshape(2 * 128, K)
        incs = jnp.dot(flat, cbuf[...], preferred_element_type=F32)
        for h in range(H):
            inc[h] = incs[:, h * W : (h + 1) * W].reshape(2, 128, W)

    with scope("c_mask"):
        loads[2].wait()
        loads[3].wait()
        for t in range(2):
            mpay[t] = jnp.where(ebuf[t : t + 1] > 0, pbuf[t], MASKED)

    with scope("d_barrier"):
        pl.semaphore_wait(barrier, 1 + NZ - 1 + 2 * (NX - 1))

    own_half = pl.ds(pl.multiple_of(core * 64, 64), 64)
    other_half = pl.ds(pl.multiple_of(other * 64, 64), 64)

    pay_copy = remote(mpay.at[:, other_half, :], pay_got, pair_s.at[0], pair_r.at[0], partner)
    inc_copy = [
        remote(inc.at[h, :, other_half, :], inc_got.at[h], pair_s.at[1 + h], pair_r.at[1 + h], partner) for h in range(H)
    ]
    pay_copy.start()
    for copy in inc_copy:
        copy.start()

    with scope("e_convert"):
        for t in range(2):
            fx_send[t] = fbuf[t, other_half, :].astype(F32)
            fall[2 * core + t] = fbuf[t, own_half, :]

    def bl_copy(h, i):
        e, dev = z_peer(i)
        return remote(bl.at[h, e], bl_all.at[h, z], bl_s.at[h, i - 1], bl_r.at[h, i - 1], dev)

    def bl_wait(h, i):
        e, dev = z_peer(i)
        src = lax.rem(z + NZ - i, NZ)
        return remote(bl.at[h, e], bl_all.at[h, src], bl_s.at[h, i - 1], bl_r.at[h, i - 1], dev)

    def fl_copy(h, i):
        e, dev = z_peer(i)
        return remote(fl.at[h, e], fl_in.at[h, z], fl_s.at[h, i - 1], fl_r.at[h, i - 1], dev)

    def fl_wait(h, i):
        e, dev = z_peer(i)
        src = lax.rem(z + NZ - i, NZ)
        return remote(fl.at[h, e], fl_in.at[h, src], fl_s.at[h, i - 1], fl_r.at[h, i - 1], dev)

    pay_copy.wait_recv()
    for h in range(H):
        with scope("f_blocks%d" % h):
            cols = pl.ds(h * W, W)
            inc_copy[h].wait_recv()
            first = core == 0
            run = jnp.zeros((64, W), F32)
            us = []
            for t in range(4):
                mine_inc, got_inc = inc[h, t % 2, own_half, :], inc_got[h, t % 2]
                mine_pay, got_pay = mpay[t % 2, own_half, cols], pay_got[t % 2, :, cols]
                own = first if t < 2 else jnp.logical_not(first)
                run = run + jnp.where(own, mine_inc, got_inc)
                us.append((jnp.where(own, mine_pay, got_pay) - run) / TEMP)
            top = functools.reduce(jnp.maximum, us)
            lse = top + jnp.log(functools.reduce(lambda p, q: p + q, [jnp.exp(u - top) for u in us]))
            for t in range(4):
                rel[h, t] = us[t]
            for s in range(NZ):
                bl[h, s, 0] = run[s * R : (s + 1) * R]
                bl[h, s, 1] = lse[s * R : (s + 1) * R]

            @pl.loop(1, NZ)
            def _(i):
                bl_copy(h, i).start()

            bl_all[h, z] = bl[h, z]

    fx_copy = remote(fx_send, fx_got, pair_s.at[3], pair_r.at[3], partner)
    fx_copy.start()
    with scope("g_features"):
        fx_copy.wait_recv()
        for t in range(2):
            fall[2 * other + t] = fx_got[t].astype(BF16)
        for k in range(8):
            strip = fall[:, :, k * 256 : (k + 1) * 256].reshape(256, 256).T
            for which in range(2):
                ft[which, k * 128 : (k + 1) * 128, :] = strip[which * 128 : (which + 1) * 128]

    stat[0] = jnp.zeros((R, C), F32)
    for h in range(H):
        with scope("h_blwait%d" % h):

            @pl.loop(1, NZ)
            def _(i):
                bl_wait(h, i).wait_recv()

        with scope("i_owner%d" % h):
            cols = slice(h * W, (h + 1) * W)
            before = jnp.zeros((R, W), F32)
            befores, ss = [], []
            for s in range(NZ):
                shift = before / TEMP
                befores.append(shift)
                ss.append(bl_all[h, s, 1] - shift)
                before = before + bl_all[h, s, 0]
            peak = functools.reduce(jnp.maximum, ss)
            lse = peak + jnp.log(functools.reduce(lambda p, q: p + q, [jnp.exp(s - peak) for s in ss]))
            later = jnp.zeros((R, W), F32)
            for s in reversed(range(NZ)):
                fl[h, s, 0] = lse + befores[s]
                fl[h, s, 1] = later
                later = later + jnp.exp(ss[s] - lse)
            smoothed = TEMP * lse
            stat[0, 0:1, cols] = jnp.sum(smoothed, axis=0, keepdims=True)
            stat[0, 1:2, cols] = jnp.sum(smoothed * smoothed, axis=0, keepdims=True)

            @pl.loop(1, NZ)
            def _(i):
                fl_copy(h, i).start()

            fl_in[h, z] = fl[h, z]

    stat_pair = remote(stat.at[0], stat_c, stat_s.at[0], stat_r.at[0], partner)
    stat_pair.start()

    def half_copy(h, j):
        chunk = lax.rem(a_other + ORDER[j], NX)
        return remote(other_part.at[h, chunk], other_got.at[h, chunk], half_s.at[h, j], half_r.at[h, j], partner)

    def half_wait(h, j):
        chunk = lax.rem(a + ORDER[j], NX)
        return remote(other_part.at[h, chunk], other_got.at[h, chunk], half_s.at[h, j], half_r.at[h, j], partner)

    lo, hi = pl.ds(0, NY // 2), pl.ds(NY // 2, NY // 2)
    two_on = lax.rem(a + 2, NX)
    one_on = lax.rem(a + 1, NX)
    one_back = lax.rem(a + 3, NX)

    def one_copies(h):
        return dict(
            via_r=remote(part.at[h, two_on, lo], via_l.at[h], one_s.at[h, 0], one_r.at[h, 0], right),
            via_l=remote(part.at[h, two_on, hi], via_r.at[h], one_s.at[h, 1], one_r.at[h, 1], left),
            direct_r=remote(part.at[h, one_on, hi], got_l.at[h, hi], one_s.at[h, 2], one_r.at[h, 2], right),
            direct_l=remote(part.at[h, one_back, lo], got_r.at[h, lo], one_s.at[h, 3], one_r.at[h, 3], left),
            comb_r=remote(part.at[h, one_on, lo], got_l.at[h, lo], one_s.at[h, 4], one_r.at[h, 4], right),
            comb_l=remote(part.at[h, one_back, hi], got_r.at[h, hi], one_s.at[h, 5], one_r.at[h, 5], left),
        )

    one = [one_copies(h) for h in range(H)]

    def product(h, which, tail, out):
        for n in range(2):
            block = jnp.dot(ft[which, n * 512 : (n + 1) * 512, :], tail, preferred_element_type=F32)
            for k in range(4):
                for p in range(NX):
                    for q in range(NY):
                        row = k * 128 + (p * NY + q) * R
                        out[h, (1 - which) * p + which * q, (1 - which) * q + which * p, n * 4 + k] = block[row : row + R]

    for h in range(H):
        with scope("j_flwait%d" % h):

            @pl.loop(1, NZ)
            def _(i):
                fl_wait(h, i).wait_recv()

        with scope("k_mm2a%d" % h):
            level = fl_in[h, :, 0].reshape(64, W)
            run = fl_in[h, :, 1].reshape(64, W)
            tails = [None] * 4
            for t in reversed(range(4)):
                run = run + jnp.exp(rel[h, t] - level)
                tails[t] = run.astype(BF16)
            tail = jnp.concatenate(tails, axis=0)
            product(h, other, tail, other_part)
            for j in range(NX):
                half_copy(h, j).start()
        with scope("l_mm2b%d" % h):
            product(h, core, tail, part)
        with scope("m_half%d" % h):
            half_wait(h, 0).wait_recv()
            part[h, two_on] = part[h, two_on] + other_got[h, two_on]
            one[h]["via_r"].start()
            one[h]["via_l"].start()
            half_wait(h, 1).wait_recv()
            part[h, one_on] = part[h, one_on] + other_got[h, one_on]
            one[h]["direct_r"].start()
            half_wait(h, 2).wait_recv()
            part[h, one_back] = part[h, one_back] + other_got[h, one_back]
            one[h]["direct_l"].start()

    def stat_copy(level, got, peer, slot, base, i):
        return remote(stat.at[level], got.at[slot], stat_s.at[base + i], stat_r.at[base + i], peer(i)[1])

    def stat_x(i, arriving=False):
        return stat_copy(1, stat_1, x_peer, lax.rem(x + NX - i, NX) if arriving else x, 0, i)

    def stat_y(i, arriving=False):
        return stat_copy(2, stat_2, y_peer, lax.rem(y + NY - i, NY) if arriving else y, 3, i)

    def stat_z(i, arriving=False):
        return stat_copy(3, stat_3, z_peer, lax.rem(z + NZ - i, NZ) if arriving else z, 6, i)

    def summed(got, n):
        return functools.reduce(lambda p, q: p + q, [got[i] for i in range(n)])

    stat_pair.wait_recv()
    stat[1] = stat[0] + stat_c[...]

    @pl.loop(1, NX)
    def _(i):
        stat_x(i).start()

    for h in range(H):
        with scope("n_via%d" % h):
            one[h]["via_r"].wait_recv()
            part[h, one_on, lo] = part[h, one_on, lo] + via_l[h]
            one[h]["comb_r"].start()
            one[h]["via_l"].wait_recv()
            part[h, one_back, hi] = part[h, one_back, hi] + via_r[h]
            one[h]["comb_l"].start()

    def two_copy(h, i):
        e, dev = b_peer(i)
        return remote(sum1.at[h, e], got2.at[h, i - 1], two_s.at[h, i - 1], two_r.at[h, i - 1], dev)

    def three_copy(h, i):
        e, dev = z_peer(i)
        return remote(sum2.at[h, e], got3.at[h, i - 1], three_s.at[h, i - 1], three_r.at[h, i - 1], dev)

    for h in range(H):
        with scope("o_one%d" % h):
            half_wait(h, 3).wait_recv()
            for name in ("direct_r", "direct_l", "comb_r", "comb_l"):
                one[h][name].wait_recv()
            sum1[h] = (part[h, a] + other_got[h, a]) + (got_l[h] + got_r[h])

            @pl.loop(1, NX)
            def _(i):
                two_copy(h, i).start()

    @pl.loop(1, NX)
    def _(i):
        stat_x(i, True).wait_recv()

    stat_1[x] = stat[1]
    stat[2] = summed(stat_1, NX)

    @pl.loop(1, NX)
    def _(i):
        stat_y(i).start()

    for h in range(H):
        with scope("p_two%d" % h):

            @pl.loop(1, NX)
            def _(i):
                two_copy(h, i).wait_recv()

            sum2[h] = (sum1[h, b] + got2[h, 0]) + (got2[h, 1] + got2[h, 2])

            @pl.loop(1, NZ)
            def _(i):
                three_copy(h, i).start()

    @pl.loop(1, NX)
    def _(i):
        stat_y(i, True).wait_recv()

    stat_2[y] = stat[2]
    stat[3] = summed(stat_2, NY)

    @pl.loop(1, NZ)
    def _(i):
        stat_z(i).start()

    for h in range(H):
        with scope("q_three%d" % h):

            @pl.loop(1, NZ)
            def _(i):
                three_copy(h, i).wait_recv()

            total = sum2[h, z]
            for i in range(NZ - 1):
                total = total + got3[h, i]
            grad[:, h * W : (h + 1) * W] = total * (-1.0 / PATHS)

    with scope("r_stat"):

        @pl.loop(1, NZ)
        def _(i):
            stat_z(i, True).wait_recv()

        stat_3[z] = stat[3]
        sums_out[...] = summed(stat_3, NZ)

    with scope("s_drain"):
        pay_copy.wait_send()
        fx_copy.wait_send()
        stat_pair.wait_send()
        for h in range(H):
            inc_copy[h].wait_send()
            for j in range(NX):
                half_copy(h, j).wait_send()
            for copy in one[h].values():
                copy.wait_send()

            @pl.loop(1, NZ)
            def _(i):
                bl_copy(h, i).wait_send()
                fl_copy(h, i).wait_send()
                three_copy(h, i).wait_send()

            @pl.loop(1, NX)
            def _(i):
                two_copy(h, i).wait_send()

        @pl.loop(1, NX)
        def _(i):
            stat_x(i).wait_send()
            stat_y(i).wait_send()

        @pl.loop(1, NZ)
        def _(i):
            stat_z(i).wait_send()


def finish(raw, sums, grad, bound, spread):
    mean = sums[0:1] * (1.0 / PATHS)
    grad[...] = raw[...]
    bound[...] = mean
    spread[...] = sums[1:2] * (1.0 / PATHS) - mean * mean


def shards(features, payoff, coefficients, exercise):
    dma = pltpu.SemaphoreType.DMA
    vmem = pltpu.VMEM
    arguments = [
        pltpu.with_memory_space_constraint(v, pltpu.HBM) for v in (features, payoff, coefficients, exercise)
    ]
    raw, sums = pl.pallas_call(
        body,
        name="dual_bound",
        out_shape=(jax.ShapeDtypeStruct((R, C), F32), jax.ShapeDtypeStruct((R, C), F32)),
        in_specs=[pl.BlockSpec(memory_space=pltpu.MemorySpace.HBM)] * 4,
        out_specs=[pl.BlockSpec(memory_space=pltpu.VMEM)] * 2,
        scratch_shapes=[
            vmem((2, 128, K), BF16),
            vmem((K, C), BF16),
            vmem((2, 128, C), F32),
            vmem((2, C), jnp.int32),
            vmem((2, 128, C), F32),
            vmem((2, 64, C), F32),
            vmem((H, 2, 128, W), F32),
            vmem((H, 2, 64, W), F32),
            vmem((2, 64, K), F32),
            vmem((2, 64, K), F32),
            vmem((4, 64, K), BF16),
            vmem((2, K // 2, 256), BF16),
            vmem((H, 4, 64, W), F32),
            vmem((H, NZ, 2, R, W), F32),
            vmem((H, NZ, 2, R, W), F32),
            vmem((H, NZ, 2, R, W), F32),
            vmem((H, NZ, 2, R, W), F32),
            vmem((H, NX, NY, NZ, R, W), F32),
            vmem((H, NX, NY, NZ, R, W), F32),
            vmem((H, NX, NY, NZ, R, W), F32),
            vmem((H, NY // 2, NZ, R, W), F32),
            vmem((H, NY // 2, NZ, R, W), F32),
            vmem((H, NY, NZ, R, W), F32),
            vmem((H, NY, NZ, R, W), F32),
            vmem((H, NY, NZ, R, W), F32),
            vmem((H, NY - 1, NZ, R, W), F32),
            vmem((H, NZ, R, W), F32),
            vmem((H, NZ - 1, R, W), F32),
            vmem((4, R, C), F32),
            vmem((R, C), F32),
            vmem((NX, R, C), F32),
            vmem((NY, R, C), F32),
            vmem((NZ, R, C), F32),
            dma((4,)),
            dma((4,)),
            dma((4,)),
            dma((H, NZ - 1)),
            dma((H, NZ - 1)),
            dma((H, NZ - 1)),
            dma((H, NZ - 1)),
            dma((H, NX)),
            dma((H, NX)),
            dma((H, 6)),
            dma((H, 6)),
            dma((H, NY - 1)),
            dma((H, NY - 1)),
            dma((H, NZ - 1)),
            dma((H, NZ - 1)),
            dma((14,)),
            dma((14,)),
        ],
        compiler_params=pltpu.CompilerParams(
            collective_id=0, has_side_effects=True, vmem_limit_bytes=40 * 1024 * 1024
        ),
    )(*arguments)
    grad, bound, spread = pl.pallas_call(
        finish,
        name="finish",
        out_shape=(
            jax.ShapeDtypeStruct((R, C), F32),
            jax.ShapeDtypeStruct((1, C), F32),
            jax.ShapeDtypeStruct((1, C), F32),
        ),
        compiler_params=pltpu.CompilerParams(vmem_limit_bytes=1024 * 1024),
    )(raw, sums)
    return grad, bound.reshape(C), spread.reshape(C)


def solution(mesh):
    torus = Mesh(mesh.devices.reshape(NZ, NC, NX, NY), AXES)
    in_specs = (P(DATE, PATH, None), P(DATE, PATH, None), P(), P(DATE, None))
    out_specs = (P(DATE + PATH, None), P(), P())
    return jax.shard_map(
        shards, mesh=torus, in_specs=in_specs, out_specs=out_specs, check_vma=False
    )
```

```python
import functools

import jax
import jax.numpy as jnp
from jax import lax
from jax.experimental import pallas as pl
from jax.experimental.pallas import tpu as pltpu
from jax.sharding import Mesh
from jax.sharding import PartitionSpec as P

DATE = ("z", "core")
PATH = ("x", "y")
AXES = ("z", "core", "x", "y")
NZ, NC, NX, NY = 8, 2, 4, 4
TEMP = 0.25
MASKED = -1e30 * TEMP
PATHS = 2048
K = 2048
C = 256
R = 8
H = 2
W = C // H
F32 = jnp.float32
BF16 = jnp.bfloat16
MESH = pl.DeviceIdType.MESH
PIECES = 2
ORDER = (2, 1, 3, 0)
FAR_FIRST = (4, 3, 5, 2, 6, 1, 7)


def scope(name):
    return jax.named_scope(name)


def body(
    feat,
    pay,
    coef,
    exer,
    grad,
    sums_out,
    fbuf,
    cbuf,
    pbuf,
    ebuf,
    mpay,
    pay_got,
    inc,
    inc_got,
    fx_send,
    fx_got,
    fall,
    ft,
    rel,
    bl,
    bl_all,
    fl,
    fl_in,
    other_part,
    other_got,
    part,
    via_l,
    via_r,
    got_l,
    got_r,
    sum1,
    got2,
    sum2,
    got3,
    stat,
    stat_c,
    stat_1,
    stat_2,
    stat_3,
    load_sem,
    send,
    pair_s,
    pair_r,
    bl_r,
    fl_r,
    half_r,
    one_r,
    two_r,
    three_r,
    stat_r,
):
    z, core, x, y = (lax.axis_index(a) for a in AXES)
    other = 1 - core

    a = (1 - core) * x + core * y
    b = (1 - core) * y + core * x
    a_other = (1 - other) * x + other * y

    def along_a(e):
        return (z, core, (1 - core) * e + core * x, (1 - core) * y + core * e)

    def along_b(e):
        return (z, core, (1 - core) * x + core * e, (1 - core) * e + core * y)

    partner = (z, other, x, y)
    right, left = along_a(lax.rem(a + 1, NX)), along_a(lax.rem(a + NX - 1, NX))

    def b_peer(i):
        e = lax.rem(b + i, NX)
        return e, along_b(e)

    def z_peer(i):
        e = lax.rem(z + i, NZ)
        return e, (e, core, x, y)

    def x_peer(i):
        e = lax.rem(x + i, NX)
        return e, (z, core, e, y)

    def y_peer(i):
        e = lax.rem(y + i, NY)
        return e, (z, core, x, e)

    def remote(src, dst, ssem, rsem, device):
        return pltpu.make_async_remote_copy(src, dst, ssem, rsem, device_id=device, device_id_type=MESH)

    def greet(device):
        pl.semaphore_signal(barrier, inc=1, device_id=device, device_id_type=MESH)

    barrier = pltpu.get_barrier_semaphore()
    with scope("a_signal"):
        for i in FAR_FIRST:
            greet(z_peer(i)[1])
        for i in (2, 1, 3):
            greet(x_peer(i)[1])
            greet(y_peer(i)[1])
        greet(partner)

    depth = K // PIECES

    def piece(n):
        return slice(n * depth, (n + 1) * depth)

    loads = []
    for n in range(PIECES):
        loads.append(pltpu.make_async_copy(coef.at[piece(n), :], cbuf.at[piece(n), :], load_sem.at[2 * n]))
        loads.append(pltpu.make_async_copy(feat.at[:, :, piece(n)], fbuf.at[:, :, piece(n)], load_sem.at[2 * n + 1]))
    loads.append(pltpu.make_async_copy(exer, ebuf, load_sem.at[2 * PIECES]))
    loads.append(pltpu.make_async_copy(pay, pbuf, load_sem.at[2 * PIECES + 1]))
    for copy in loads:
        copy.start()

    with scope("b_mm1"):
        incs = None
        for n in range(PIECES):
            loads[2 * n].wait()
            loads[2 * n + 1].wait()
            flat = fbuf[:, :, piece(n)].reshape(2 * 128, depth)
            term = jnp.dot(flat, cbuf[piece(n), :], preferred_element_type=F32)
            incs = term if incs is None else incs + term
        for h in range(H):
            inc[h] = incs[:, h * W : (h + 1) * W].reshape(2, 128, W)

    with scope("c_mask"):
        loads[2 * PIECES].wait()
        loads[2 * PIECES + 1].wait()
        for t in range(2):
            mpay[t] = jnp.where(ebuf[t : t + 1] > 0, pbuf[t], MASKED)

    with scope("d_barrier"):
        pl.semaphore_wait(barrier, 1 + NZ - 1 + 2 * (NX - 1))

    own_half = pl.ds(pl.multiple_of(core * 64, 64), 64)
    other_half = pl.ds(pl.multiple_of(other * 64, 64), 64)

    pay_copy = remote(mpay.at[:, other_half, :], pay_got, pair_s.at[0], pair_r.at[0], partner)
    inc_copy = [
        remote(inc.at[h, :, other_half, :], inc_got.at[h], pair_s.at[1], pair_r.at[1 + h], partner) for h in range(H)
    ]
    pay_copy.start()
    for copy in inc_copy:
        copy.start()

    with scope("e_convert"):
        for t in range(2):
            fx_send[t] = fbuf[t, other_half, :].astype(F32)
            fall[2 * core + t] = fbuf[t, own_half, :]

    def bl_copy(h, i):
        e, dev = z_peer(i)
        return remote(bl.at[h, e], bl_all.at[h, i], send.at[0], bl_r.at[h], dev)

    def fl_copy(h, i):
        e, dev = z_peer(i)
        return remote(fl.at[h, e], fl_in.at[h, i], send.at[1], fl_r.at[h], dev)

    def arrived(ref, sem):
        pltpu.make_async_copy(ref, ref, sem).wait()

    def from_z(s):
        return lax.rem(z + NZ - s, NZ)

    pay_copy.wait_recv()
    for h in range(H):
        with scope("f_blocks%d" % h):
            cols = pl.ds(h * W, W)
            inc_copy[h].wait_recv()
            first = core == 0
            run = jnp.zeros((64, W), F32)
            us = []
            for t in range(4):
                mine_inc, got_inc = inc[h, t % 2, own_half, :], inc_got[h, t % 2]
                mine_pay, got_pay = mpay[t % 2, own_half, cols], pay_got[t % 2, :, cols]
                own = first if t < 2 else jnp.logical_not(first)
                run = run + jnp.where(own, mine_inc, got_inc)
                us.append((jnp.where(own, mine_pay, got_pay) - run) / TEMP)
            top = functools.reduce(jnp.maximum, us)
            lse = top + jnp.log(functools.reduce(lambda p, q: p + q, [jnp.exp(u - top) for u in us]))
            for t in range(4):
                rel[h, t] = us[t]
            for s in range(NZ):
                bl[h, s, 0] = run[s * R : (s + 1) * R]
                bl[h, s, 1] = lse[s * R : (s + 1) * R]

            for i in FAR_FIRST:
                bl_copy(h, i).start()

            bl_all[h, 0] = bl[h, z]

    fx_copy = remote(fx_send, fx_got, pair_s.at[2], pair_r.at[3], partner)
    fx_copy.start()
    with scope("g_features"):
        fx_copy.wait_recv()
        for t in range(2):
            fall[2 * other + t] = fx_got[t].astype(BF16)
        for k in range(8):
            strip = fall[:, :, k * 256 : (k + 1) * 256].reshape(256, 256).T
            for which in range(2):
                ft[which, k * 128 : (k + 1) * 128, :] = strip[which * 128 : (which + 1) * 128]

    stat[0] = jnp.zeros((R, C), F32)
    for h in range(H):
        with scope("h_blwait%d" % h):

            arrived(bl_all.at[h, pl.ds(1, NZ - 1)], bl_r.at[h])

        with scope("i_owner%d" % h):
            cols = slice(h * W, (h + 1) * W)
            before = jnp.zeros((R, W), F32)
            befores, ss = [], []
            for s in range(NZ):
                shift = before / TEMP
                befores.append(shift)
                ss.append(bl_all[h, from_z(s), 1] - shift)
                before = before + bl_all[h, from_z(s), 0]
            peak = functools.reduce(jnp.maximum, ss)
            lse = peak + jnp.log(functools.reduce(lambda p, q: p + q, [jnp.exp(s - peak) for s in ss]))
            later = jnp.zeros((R, W), F32)
            for s in reversed(range(NZ)):
                fl[h, s, 0] = lse + befores[s]
                fl[h, s, 1] = later
                later = later + jnp.exp(ss[s] - lse)
            smoothed = TEMP * lse
            stat[0, 0:1, cols] = jnp.sum(smoothed, axis=0, keepdims=True)
            stat[0, 1:2, cols] = jnp.sum(smoothed * smoothed, axis=0, keepdims=True)

            for i in FAR_FIRST:
                fl_copy(h, i).start()

            fl_in[h, 0] = fl[h, z]

    def stat_x(i):
        return remote(stat.at[0], stat_1.at[i], send.at[2], stat_r.at[0], x_peer(i)[1])

    def stat_y(i):
        return remote(stat.at[1], stat_2.at[i], send.at[2], stat_r.at[1], y_peer(i)[1])

    def stat_z(i):
        return remote(stat.at[2], stat_3.at[i], send.at[3], stat_r.at[2], z_peer(i)[1])

    def summed(got, here, n):
        return functools.reduce(lambda p, q: p + q, [got[lax.rem(here + n - s, n)] for s in range(n)])

    stat_1[0] = stat[0]
    for i in (2, 1, 3):
        stat_x(i).start()

    stat_pair = remote(stat.at[3], stat_c, send.at[2], stat_r.at[3], partner)

    def half_copy(h, j):
        chunk = lax.rem(a_other + ORDER[j], NX)
        return remote(other_part.at[h, chunk], other_got.at[h, j], send.at[4], half_r.at[h, min(j, 1)], partner)

    lo, hi = pl.ds(0, NY // 2), pl.ds(NY // 2, NY // 2)
    two_on = lax.rem(a + 2, NX)
    one_on = lax.rem(a + 1, NX)
    one_back = lax.rem(a + 3, NX)

    def one_copies(h):
        return dict(
            via_r=remote(part.at[h, two_on, lo], via_l.at[h], send.at[5], one_r.at[h, 0], right),
            via_l=remote(part.at[h, two_on, hi], via_r.at[h], send.at[5], one_r.at[h, 1], left),
            direct_r=remote(part.at[h, one_on, hi], got_l.at[h, hi], send.at[5], one_r.at[h, 2], right),
            direct_l=remote(part.at[h, one_back, lo], got_r.at[h, lo], send.at[5], one_r.at[h, 3], left),
            comb_r=remote(part.at[h, one_on, lo], got_l.at[h, lo], send.at[5], one_r.at[h, 2], right),
            comb_l=remote(part.at[h, one_back, hi], got_r.at[h, hi], send.at[5], one_r.at[h, 3], left),
        )

    one = [one_copies(h) for h in range(H)]

    def product(h, which, tail, out):
        for n in range(2):
            block = jnp.dot(ft[which, n * 512 : (n + 1) * 512, :], tail, preferred_element_type=F32)
            for k in range(4):
                for p in range(NX):
                    for q in range(NY):
                        row = k * 128 + (p * NY + q) * R
                        out[h, (1 - which) * p + which * q, (1 - which) * q + which * p, n * 4 + k] = block[row : row + R]

    for h in range(H):
        with scope("j_flwait%d" % h):

            arrived(fl_in.at[h, pl.ds(1, NZ - 1)], fl_r.at[h])

        with scope("k_mm2a%d" % h):
            level = jnp.concatenate([fl_in[h, from_z(s), 0] for s in range(NZ)], axis=0)
            run = jnp.concatenate([fl_in[h, from_z(s), 1] for s in range(NZ)], axis=0)
            tails = [None] * 4
            for t in reversed(range(4)):
                run = run + jnp.exp(rel[h, t] - level)
                tails[t] = run.astype(BF16)
            tail = jnp.concatenate(tails, axis=0)
            product(h, other, tail, other_part)
            for j in range(NX):
                half_copy(h, j).start()
        with scope("l_mm2b%d" % h):
            product(h, core, tail, part)
        if h == 0:
            arrived(stat_1.at[pl.ds(1, NX - 1)], stat_r.at[0])
            stat[1] = summed(stat_1, x, NX)
            stat_2[0] = stat[1]
            for i in (2, 1, 3):
                stat_y(i).start()

    def joined(h, j):
        chunk = lax.rem(a + ORDER[j], NX)
        part[h, chunk] = part[h, chunk] + other_got[h, j]

    def begin(h):
        with scope("m_half%d" % h):
            arrived(other_got.at[h, 0], half_r.at[h, 0])
            joined(h, 0)
            one[h]["via_r"].start()
            one[h]["via_l"].start()

    def direct(h):
        with scope("n_direct%d" % h):
            arrived(other_got.at[h, pl.ds(1, NX - 1)], half_r.at[h, 1])
            joined(h, 1)
            one[h]["direct_r"].start()
            joined(h, 2)
            one[h]["direct_l"].start()

    def combine(h):
        with scope("n_via%d" % h):
            one[h]["via_r"].wait_recv()
            part[h, one_on, lo] = part[h, one_on, lo] + via_l[h]
            one[h]["comb_r"].start()
            one[h]["via_l"].wait_recv()
            part[h, one_back, hi] = part[h, one_back, hi] + via_r[h]
            one[h]["comb_l"].start()

    begin(0)
    direct(0)
    begin(1)
    combine(0)
    direct(1)
    with scope("o_stat"):
        arrived(stat_2.at[pl.ds(1, NY - 1)], stat_r.at[1])
        stat[2] = summed(stat_2, y, NY)
        stat_3[0] = stat[2]
        for i in FAR_FIRST:
            stat_z(i).start()
    combine(1)

    def two_copy(h, i):
        e, dev = b_peer(i)
        return remote(sum1.at[h, e], got2.at[h, i - 1], send.at[6], two_r.at[h], dev)

    def three_copy(h, i):
        e, dev = z_peer(i)
        return remote(sum2.at[h, e], got3.at[h, i - 1], send.at[7], three_r.at[h], dev)

    for h in range(H):
        with scope("o_one%d" % h):
            arrived(got_l.at[h], one_r.at[h, 2])
            arrived(got_r.at[h], one_r.at[h, 3])
            sum1[h] = (part[h, a] + other_got[h, 3]) + (got_l[h] + got_r[h])
            for i in (2, 1, 3):
                two_copy(h, i).start()

    for h in range(H):
        with scope("p_two%d" % h):
            arrived(got2.at[h], two_r.at[h])
            sum2[h] = (sum1[h, b] + got2[h, 0]) + (got2[h, 1] + got2[h, 2])

            for i in FAR_FIRST:
                three_copy(h, i).start()

    with scope("q_stat"):
        arrived(stat_3.at[pl.ds(1, NZ - 1)], stat_r.at[2])
        stat[3] = summed(stat_3, z, NZ)
        stat_pair.start()

    for h in range(H):
        with scope("q_three%d" % h):
            arrived(got3.at[h], three_r.at[h])
            total = sum2[h, z]
            for i in range(NZ - 1):
                total = total + got3[h, i]
            grad[:, h * W : (h + 1) * W] = total * (-1.0 / PATHS)

    with scope("r_stat"):
        arrived(stat_c, stat_r.at[3])
        sums_out[...] = stat[3] + stat_c[...]

    with scope("s_drain"):
        pay_copy.wait_send()
        arrived(inc_got, pair_s.at[1])
        fx_copy.wait_send()
        arrived(bl.at[:, pl.ds(0, NZ - 1)], send.at[0])
        arrived(fl.at[:, pl.ds(0, NZ - 1)], send.at[1])
        arrived(stat_3.at[pl.ds(0, 7)], send.at[2])
        arrived(stat_3.at[pl.ds(0, 7)], send.at[3])
        arrived(other_part, send.at[4])
        arrived(part.at[:, pl.ds(0, NX - 1)], send.at[5])
        arrived(sum1.at[:, pl.ds(0, NY - 1)], send.at[6])
        arrived(sum2.at[:, pl.ds(0, NZ - 1)], send.at[7])


def finish(raw, sums, grad, bound, spread):
    mean = sums[0:1] * (1.0 / PATHS)
    grad[...] = raw[...]
    bound[...] = mean
    spread[...] = sums[1:2] * (1.0 / PATHS) - mean * mean


def shards(features, payoff, coefficients, exercise):
    dma = pltpu.SemaphoreType.DMA
    vmem = pltpu.VMEM
    arguments = [
        pltpu.with_memory_space_constraint(v, pltpu.HBM) for v in (features, payoff, coefficients, exercise)
    ]
    raw, sums = pl.pallas_call(
        body,
        name="dual_bound",
        out_shape=(jax.ShapeDtypeStruct((R, C), F32), jax.ShapeDtypeStruct((R, C), F32)),
        in_specs=[pl.BlockSpec(memory_space=pltpu.MemorySpace.HBM)] * 4,
        out_specs=[pl.BlockSpec(memory_space=pltpu.VMEM)] * 2,
        scratch_shapes=[
            vmem((2, 128, K), BF16),
            vmem((K, C), BF16),
            vmem((2, 128, C), F32),
            vmem((2, C), jnp.int32),
            vmem((2, 128, C), F32),
            vmem((2, 64, C), F32),
            vmem((H, 2, 128, W), F32),
            vmem((H, 2, 64, W), F32),
            vmem((2, 64, K), F32),
            vmem((2, 64, K), F32),
            vmem((4, 64, K), BF16),
            vmem((2, K // 2, 256), BF16),
            vmem((H, 4, 64, W), F32),
            vmem((H, NZ, 2, R, W), F32),
            vmem((H, NZ, 2, R, W), F32),
            vmem((H, NZ, 2, R, W), F32),
            vmem((H, NZ, 2, R, W), F32),
            vmem((H, NX, NY, NZ, R, W), F32),
            vmem((H, NX, NY, NZ, R, W), F32),
            vmem((H, NX, NY, NZ, R, W), F32),
            vmem((H, NY // 2, NZ, R, W), F32),
            vmem((H, NY // 2, NZ, R, W), F32),
            vmem((H, NY, NZ, R, W), F32),
            vmem((H, NY, NZ, R, W), F32),
            vmem((H, NY, NZ, R, W), F32),
            vmem((H, NY - 1, NZ, R, W), F32),
            vmem((H, NZ, R, W), F32),
            vmem((H, NZ - 1, R, W), F32),
            vmem((4, R, C), F32),
            vmem((R, C), F32),
            vmem((NX, R, C), F32),
            vmem((NY, R, C), F32),
            vmem((NZ, R, C), F32),
            dma((2 * PIECES + 2,)),
            dma((8,)),
            dma((3,)),
            dma((4,)),
            dma((H,)),
            dma((H,)),
            dma((H, 2)),
            dma((H, 4)),
            dma((H,)),
            dma((H,)),
            dma((4,)),
        ],
        compiler_params=pltpu.CompilerParams(
            collective_id=0, has_side_effects=True, vmem_limit_bytes=40 * 1024 * 1024
        ),
    )(*arguments)
    grad, bound, spread = pl.pallas_call(
        finish,
        name="finish",
        out_shape=(
            jax.ShapeDtypeStruct((R, C), F32),
            jax.ShapeDtypeStruct((1, C), F32),
            jax.ShapeDtypeStruct((1, C), F32),
        ),
        compiler_params=pltpu.CompilerParams(vmem_limit_bytes=1024 * 1024),
    )(raw, sums)
    return grad, bound.reshape(C), spread.reshape(C)


def solution(mesh):
    torus = Mesh(mesh.devices.reshape(NZ, NC, NX, NY), AXES)
    in_specs = (P(DATE, PATH, None), P(DATE, PATH, None), P(), P(DATE, None))
    out_specs = (P(DATE + PATH, None), P(), P())
    return jax.shard_map(
        shards, mesh=torus, in_specs=in_specs, out_specs=out_specs, check_vma=False
    )
```

```python
import functools

import jax
import jax.numpy as jnp
from jax import lax
from jax.experimental import pallas as pl
from jax.experimental.pallas import tpu as pltpu
from jax.sharding import Mesh
from jax.sharding import PartitionSpec as P

DATE = ("z", "core")
PATH = ("x", "y")
AXES = ("z", "core", "x", "y")
NZ, NC, NX, NY = 8, 2, 4, 4
TEMP = 0.25
MASKED = -1e30 * TEMP
PATHS = 2048
K = 2048
C = 256
R = 8
H = 2
W = C // H
F32 = jnp.float32
BF16 = jnp.bfloat16
MESH = pl.DeviceIdType.MESH
PIECES = 2
FAR_FIRST = (4, 3, 5, 2, 6, 1, 7)


def scope(name):
    return jax.named_scope(name)


def body(
    feat,
    pay,
    coef,
    exer,
    grad,
    sums_out,
    fbuf,
    cbuf,
    pbuf,
    ebuf,
    both,
    both_got,
    fx_send,
    fall,
    ft32,
    ft,
    rel,
    bl,
    bl_all,
    fl,
    fl_in,
    tails,
    tail_got,
    part,
    via_l,
    via_r,
    got_l,
    got_r,
    sum1,
    got2,
    sum2,
    got3,
    stat,
    stat_c,
    stat_1,
    stat_2,
    stat_3,
    load_sem,
    send,
    pair_s,
    pair_r,
    bl_r,
    fl_r,
    half_r,
    one_r,
    two_r,
    three_r,
    stat_r,
):
    z, core, x, y = (lax.axis_index(a) for a in AXES)
    other = 1 - core

    a = (1 - core) * x + core * y
    b = (1 - core) * y + core * x
    a_other = (1 - other) * x + other * y

    def along_a(e):
        return (z, core, (1 - core) * e + core * x, (1 - core) * y + core * e)

    def along_b(e):
        return (z, core, (1 - core) * x + core * e, (1 - core) * e + core * y)

    partner = (z, other, x, y)
    right, left = along_a(lax.rem(a + 1, NX)), along_a(lax.rem(a + NX - 1, NX))

    def b_peer(i):
        e = lax.rem(b + i, NX)
        return e, along_b(e)

    def z_peer(i):
        e = lax.rem(z + i, NZ)
        return e, (e, core, x, y)

    def x_peer(i):
        e = lax.rem(x + i, NX)
        return e, (z, core, e, y)

    def y_peer(i):
        e = lax.rem(y + i, NY)
        return e, (z, core, x, e)

    def remote(src, dst, ssem, rsem, device):
        return pltpu.make_async_remote_copy(src, dst, ssem, rsem, device_id=device, device_id_type=MESH)

    def greet(device):
        pl.semaphore_signal(barrier, inc=1, device_id=device, device_id_type=MESH)

    barrier = pltpu.get_barrier_semaphore()
    with scope("a_signal"):
        for i in FAR_FIRST:
            greet(z_peer(i)[1])
        for i in (2, 1, 3):
            greet(x_peer(i)[1])
            greet(y_peer(i)[1])
        greet(partner)

    depth = K // PIECES

    def piece(n):
        return slice(n * depth, (n + 1) * depth)

    loads = []
    for n in range(PIECES):
        loads.append(pltpu.make_async_copy(coef.at[piece(n), :], cbuf.at[piece(n), :], load_sem.at[2 * n]))
        loads.append(pltpu.make_async_copy(feat.at[:, :, piece(n)], fbuf.at[:, :, piece(n)], load_sem.at[2 * n + 1]))
    loads.append(pltpu.make_async_copy(exer, ebuf, load_sem.at[2 * PIECES]))
    loads.append(pltpu.make_async_copy(pay, pbuf, load_sem.at[2 * PIECES + 1]))
    for copy in loads:
        copy.start()

    with scope("b_mm1"):
        incs = None
        for n in range(PIECES):
            loads[2 * n].wait()
            loads[2 * n + 1].wait()
            flat = fbuf[:, :, piece(n)].reshape(2 * 128, depth)
            term = jnp.dot(flat, cbuf[piece(n), :], preferred_element_type=F32)
            incs = term if incs is None else incs + term
        for h in range(H):
            both[h, 1] = incs[:, h * W : (h + 1) * W].reshape(2, 128, W)

    with scope("c_mask"):
        loads[2 * PIECES].wait()
        loads[2 * PIECES + 1].wait()
        for t in range(2):
            masked = jnp.where(ebuf[t : t + 1] > 0, pbuf[t], MASKED)
            for h in range(H):
                both[h, 0, t] = masked[:, h * W : (h + 1) * W]

    with scope("d_barrier"):
        pl.semaphore_wait(barrier, 1 + NZ - 1 + 2 * (NX - 1))

    own_half = pl.ds(pl.multiple_of(core * 64, 64), 64)
    other_half = pl.ds(pl.multiple_of(other * 64, 64), 64)

    both_copy = [
        remote(both.at[h, :, :, other_half, :], both_got.at[h], pair_s.at[0], pair_r.at[h], partner) for h in range(H)
    ]
    for copy in both_copy:
        copy.start()

    def bl_copy(h, i):
        e, dev = z_peer(i)
        return remote(bl.at[h, e], bl_all.at[h, i], send.at[0], bl_r.at[h], dev)

    def fl_copy(h, i):
        e, dev = z_peer(i)
        return remote(fl.at[h, e], fl_in.at[h, i], send.at[1], fl_r.at[h], dev)

    def arrived(ref, sem):
        pltpu.make_async_copy(ref, ref, sem).wait()

    def from_z(s):
        return lax.rem(z + NZ - s, NZ)

    for h in range(H):
        with scope("f_blocks%d" % h):
            arrived(both_got.at[h], pair_r.at[h])
            first = core == 0
            run = jnp.zeros((64, W), F32)
            us = []
            for t in range(4):
                mine_pay, got_pay = both[h, 0, t % 2, own_half, :], both_got[h, 0, t % 2]
                mine_inc, got_inc = both[h, 1, t % 2, own_half, :], both_got[h, 1, t % 2]
                own = first if t < 2 else jnp.logical_not(first)
                run = run + jnp.where(own, mine_inc, got_inc)
                us.append((jnp.where(own, mine_pay, got_pay) - run) / TEMP)
            top = functools.reduce(jnp.maximum, us)
            lse = top + jnp.log(functools.reduce(lambda p, q: p + q, [jnp.exp(u - top) for u in us]))
            for t in range(4):
                rel[h, t] = us[t]
            for s in range(NZ):
                bl[h, s, 0] = run[s * R : (s + 1) * R]
                bl[h, s, 1] = lse[s * R : (s + 1) * R]

            for i in FAR_FIRST:
                bl_copy(h, i).start()

            bl_all[h, 0] = bl[h, z]

    fx_copy = remote(fx_send, fall.at[pl.ds(2 * core, 2)], pair_s.at[1], pair_r.at[2], partner)

    with scope("g_convert"):
        for n in range(NZ):
            theirs = pl.ds(pl.multiple_of(n * 256 + other * 128, 128), 128)
            for t in range(2):
                fx_send[t, :, n * 128 : (n + 1) * 128] = fbuf[t, :, theirs].astype(F32)
        fx_copy.start()
        for n in range(NZ):
            ours = pl.ds(pl.multiple_of(n * 256 + core * 128, 128), 128)
            for t in range(2):
                fall[2 * core + t, :, n * 128 : (n + 1) * 128] = fbuf[t, :, ours].astype(F32)

    with scope("g_features"):
        arrived(fx_send, pair_r.at[2])
        for side, rows in enumerate((own_half, other_half)):
            for n in range(NZ):
                strip = fall[:, rows, n * 128 : (n + 1) * 128].reshape(256, 128).T
                for p in range(NX):
                    for q in range(NY):
                        row = (p * NY + q) * R
                        to_a, to_b = (1 - core) * p + core * q, (1 - core) * q + core * p
                        ft32[to_a, to_b, n] = strip[row : row + R]
            for p in range(NX):
                ft[side, p] = ft32[p].reshape(NY * NZ * R, 256).astype(BF16)

    stat[0] = jnp.zeros((R, C), F32)
    for h in range(H):
        with scope("h_blwait%d" % h):

            arrived(bl_all.at[h, pl.ds(1, NZ - 1)], bl_r.at[h])

        with scope("i_owner%d" % h):
            cols = slice(h * W, (h + 1) * W)
            before = jnp.zeros((R, W), F32)
            befores, ss = [], []
            for s in range(NZ):
                shift = before / TEMP
                befores.append(shift)
                ss.append(bl_all[h, from_z(s), 1] - shift)
                before = before + bl_all[h, from_z(s), 0]
            peak = functools.reduce(jnp.maximum, ss)
            lse = peak + jnp.log(functools.reduce(lambda p, q: p + q, [jnp.exp(s - peak) for s in ss]))
            later = jnp.zeros((R, W), F32)
            for s in reversed(range(NZ)):
                fl[h, s, 0] = lse + befores[s]
                fl[h, s, 1] = later
                later = later + jnp.exp(ss[s] - lse)
            smoothed = TEMP * lse
            stat[0, 0:1, cols] = jnp.sum(smoothed, axis=0, keepdims=True)
            stat[0, 1:2, cols] = jnp.sum(smoothed * smoothed, axis=0, keepdims=True)

            for i in FAR_FIRST:
                fl_copy(h, i).start()

            fl_in[h, 0] = fl[h, z]

    def stat_x(i):
        return remote(stat.at[0], stat_1.at[i], send.at[2], stat_r.at[0], x_peer(i)[1])

    def stat_y(i):
        return remote(stat.at[1], stat_2.at[i], send.at[2], stat_r.at[1], y_peer(i)[1])

    def stat_z(i):
        return remote(stat.at[2], stat_3.at[i], send.at[3], stat_r.at[2], z_peer(i)[1])

    def summed(got, here, n):
        return functools.reduce(lambda p, q: p + q, [got[lax.rem(here + n - s, n)] for s in range(n)])

    stat_1[0] = stat[0]
    for i in (2, 1, 3):
        stat_x(i).start()

    stat_pair = remote(stat.at[3], stat_c, send.at[2], stat_r.at[3], partner)

    tail_copy = [remote(tails.at[h], tail_got.at[h], send.at[4], half_r.at[h], partner) for h in range(H)]

    lo, hi = pl.ds(0, NY // 2), pl.ds(NY // 2, NY // 2)
    two_on = lax.rem(a + 2, NX)
    one_on = lax.rem(a + 1, NX)
    one_back = lax.rem(a + 3, NX)

    def one_copies(h):
        copies = dict(
            direct_r=remote(part.at[h, one_on, hi], got_l.at[h, hi], send.at[5], one_r.at[h, 4], right),
            direct_l=remote(part.at[h, one_back, lo], got_r.at[h, lo], send.at[5], one_r.at[h, 5], left),
        )
        for n in range(NY // 2):
            m = NY // 2 + n
            copies["via_r%d" % n] = remote(part.at[h, two_on, n], via_l.at[h, n], send.at[5], one_r.at[h, n], right)
            copies["via_l%d" % n] = remote(part.at[h, two_on, m], via_r.at[h, n], send.at[5], one_r.at[h, 2 + n], left)
            copies["comb_r%d" % n] = remote(part.at[h, one_on, n], got_l.at[h, n], send.at[5], one_r.at[h, 4], right)
            copies["comb_l%d" % n] = remote(part.at[h, one_back, m], got_r.at[h, m], send.at[5], one_r.at[h, 5], left)
        return copies

    one = [one_copies(h) for h in range(H)]

    def reverse_scan(h):
        with scope("j_flwait%d" % h):
            arrived(fl_in.at[h, pl.ds(1, NZ - 1)], fl_r.at[h])
        with scope("k_tails%d" % h):
            level = jnp.concatenate([fl_in[h, from_z(s), 0] for s in range(NZ)], axis=0)
            run = jnp.concatenate([fl_in[h, from_z(s), 1] for s in range(NZ)], axis=0)
            for t in reversed(range(4)):
                run = run + jnp.exp(rel[h, t] - level)
                tails[h, t] = run
            tail_copy[h].start()

    def own_paths(h):
        with scope("k_mm2a%d" % h):
            mine = tails[h].reshape(256, W).astype(BF16)
            for p in range(NX):
                part[h, p] = jnp.dot(ft[0, p], mine, preferred_element_type=F32).reshape(NY, NZ, R, W)

    def begin(h):
        with scope("m_half%d" % h):
            arrived(tail_got.at[h], half_r.at[h])
            theirs = tail_got[h].reshape(256, W).astype(BF16)
            for p in range(NX):
                term = jnp.dot(ft[1, p], theirs, preferred_element_type=F32)
                part[h, p] = part[h, p] + term.reshape(NY, NZ, R, W)
            for n in range(NY // 2):
                one[h]["via_r%d" % n].start()
                one[h]["via_l%d" % n].start()

    def direct(h):
        one[h]["direct_r"].start()
        one[h]["direct_l"].start()

    def combine(h):
        with scope("n_via%d" % h):
            for n in range(NY // 2):
                m = NY // 2 + n
                one[h]["via_r%d" % n].wait_recv()
                part[h, one_on, n] = part[h, one_on, n] + via_l[h, n]
                one[h]["comb_r%d" % n].start()
                one[h]["via_l%d" % n].wait_recv()
                part[h, one_back, m] = part[h, one_back, m] + via_r[h, n]
                one[h]["comb_l%d" % n].start()

    reverse_scan(0)
    own_paths(0)
    arrived(stat_1.at[pl.ds(1, NX - 1)], stat_r.at[0])
    stat[1] = summed(stat_1, x, NX)
    stat_2[0] = stat[1]
    for i in (2, 1, 3):
        stat_y(i).start()
    begin(0)
    direct(0)
    reverse_scan(1)
    own_paths(1)
    begin(1)
    combine(0)
    direct(1)
    with scope("o_stat"):
        arrived(stat_2.at[pl.ds(1, NY - 1)], stat_r.at[1])
        stat[2] = summed(stat_2, y, NY)
        stat_3[0] = stat[2]
        for i in FAR_FIRST:
            stat_z(i).start()
    combine(1)

    def two_copy(h, i):
        e, dev = b_peer(i)
        return remote(sum1.at[h, e], got2.at[h, i - 1], send.at[6], two_r.at[h], dev)

    def three_copy(h, i):
        e, dev = z_peer(i)
        return remote(sum2.at[h, e], got3.at[h, i - 1], send.at[7], three_r.at[h], dev)

    for h in range(H):
        with scope("o_one%d" % h):
            arrived(got_l.at[h], one_r.at[h, 4])
            arrived(got_r.at[h], one_r.at[h, 5])
            sum1[h] = part[h, a] + (got_l[h] + got_r[h])
            for i in (2, 1, 3):
                two_copy(h, i).start()

    for h in range(H):
        with scope("p_two%d" % h):
            arrived(got2.at[h], two_r.at[h])
            sum2[h] = (sum1[h, b] + got2[h, 0]) + (got2[h, 1] + got2[h, 2])

            for i in FAR_FIRST:
                three_copy(h, i).start()

    with scope("q_stat"):
        arrived(stat_3.at[pl.ds(1, NZ - 1)], stat_r.at[2])
        stat[3] = summed(stat_3, z, NZ)
        stat_pair.start()

    for h in range(H):
        with scope("q_three%d" % h):
            arrived(got3.at[h], three_r.at[h])
            total = sum2[h, z]
            for i in range(NZ - 1):
                total = total + got3[h, i]
            grad[:, h * W : (h + 1) * W] = total * (-1.0 / PATHS)

    with scope("r_stat"):
        arrived(stat_c, stat_r.at[3])
        sums_out[...] = stat[3] + stat_c[...]

    with scope("s_drain"):
        arrived(both_got, pair_s.at[0])
        fx_copy.wait_send()
        arrived(bl.at[:, pl.ds(0, NZ - 1)], send.at[0])
        arrived(fl.at[:, pl.ds(0, NZ - 1)], send.at[1])
        arrived(stat_3.at[pl.ds(0, 7)], send.at[2])
        arrived(stat_3.at[pl.ds(0, 7)], send.at[3])
        arrived(tails, send.at[4])
        arrived(part.at[:, pl.ds(0, NX - 1)], send.at[5])
        arrived(sum1.at[:, pl.ds(0, NY - 1)], send.at[6])
        arrived(sum2.at[:, pl.ds(0, NZ - 1)], send.at[7])


def finish(raw, sums, grad, bound, spread):
    mean = sums[0:1] * (1.0 / PATHS)
    grad[...] = raw[...]
    bound[...] = mean
    spread[...] = sums[1:2] * (1.0 / PATHS) - mean * mean


def shards(features, payoff, coefficients, exercise):
    dma = pltpu.SemaphoreType.DMA
    vmem = pltpu.VMEM
    arguments = [
        pltpu.with_memory_space_constraint(v, pltpu.HBM) for v in (features, payoff, coefficients, exercise)
    ]
    raw, sums = pl.pallas_call(
        body,
        name="dual_bound",
        out_shape=(jax.ShapeDtypeStruct((R, C), F32), jax.ShapeDtypeStruct((R, C), F32)),
        in_specs=[pl.BlockSpec(memory_space=pltpu.MemorySpace.HBM)] * 4,
        out_specs=[pl.BlockSpec(memory_space=pltpu.VMEM)] * 2,
        scratch_shapes=[
            vmem((2, 128, K), BF16),
            vmem((K, C), BF16),
            vmem((2, 128, C), F32),
            vmem((2, C), jnp.int32),
            vmem((H, 2, 2, 128, W), F32),
            vmem((H, 2, 2, 64, W), F32),
            vmem((2, 128, K // 2), F32),
            vmem((4, 128, K // 2), F32),
            vmem((NX, NY, NZ, R, 256), F32),
            vmem((2, NX, NY * NZ * R, 256), BF16),
            vmem((H, 4, 64, W), F32),
            vmem((H, NZ, 2, R, W), F32),
            vmem((H, NZ, 2, R, W), F32),
            vmem((H, NZ, 2, R, W), F32),
            vmem((H, NZ, 2, R, W), F32),
            vmem((H, 4, 64, W), F32),
            vmem((H, 4, 64, W), F32),
            vmem((H, NX, NY, NZ, R, W), F32),
            vmem((H, NY // 2, NZ, R, W), F32),
            vmem((H, NY // 2, NZ, R, W), F32),
            vmem((H, NY, NZ, R, W), F32),
            vmem((H, NY, NZ, R, W), F32),
            vmem((H, NY, NZ, R, W), F32),
            vmem((H, NY - 1, NZ, R, W), F32),
            vmem((H, NZ, R, W), F32),
            vmem((H, NZ - 1, R, W), F32),
            vmem((4, R, C), F32),
            vmem((R, C), F32),
            vmem((NX, R, C), F32),
            vmem((NY, R, C), F32),
            vmem((NZ, R, C), F32),
            dma((2 * PIECES + 2,)),
            dma((8,)),
            dma((2,)),
            dma((3,)),
            dma((H,)),
            dma((H,)),
            dma((H,)),
            dma((H, 6)),
            dma((H,)),
            dma((H,)),
            dma((4,)),
        ],
        compiler_params=pltpu.CompilerParams(
            collective_id=0, has_side_effects=True, vmem_limit_bytes=40 * 1024 * 1024
        ),
    )(*arguments)
    grad, bound, spread = pl.pallas_call(
        finish,
        name="finish",
        out_shape=(
            jax.ShapeDtypeStruct((R, C), F32),
            jax.ShapeDtypeStruct((1, C), F32),
            jax.ShapeDtypeStruct((1, C), F32),
        ),
        compiler_params=pltpu.CompilerParams(vmem_limit_bytes=1024 * 1024),
    )(raw, sums)
    return grad, bound.reshape(C), spread.reshape(C)


def solution(mesh):
    torus = Mesh(mesh.devices.reshape(NZ, NC, NX, NY), AXES)
    in_specs = (P(DATE, PATH, None), P(DATE, PATH, None), P(), P(DATE, None))
    out_specs = (P(DATE + PATH, None), P(), P())
    return jax.shard_map(
        shards, mesh=torus, in_specs=in_specs, out_specs=out_specs, check_vma=False
    )
```
